32 devices in a mesh: groups: 2 (over x), row: 16 (over z, y, core).
Axes of the slice: x: 2, y: 2, z: 4, core: 2. Of those that a mesh axis runs over, the one named last changes fastest.
Arguments:
- source_slab: bfloat16 [256, 4096], P(('groups', 'row')), parts along dimension 0, may hold values from -40 to 40
- slab_index: int32 [2], P('groups'), parts along dimension 0, may hold values from 0 to 127
- cache_slot: int32 [256], P('groups'), parts along dimension 0, may hold values from 0 to 127, each once
- ffn_gain: float32 [4096], replicated, may hold values from 0.1 to 1.9
- gate_weight: bfloat16 [4096, 16384], P(None, 'row'), may hold values from -0.09375 to 0.09375
- up_weight: bfloat16 [4096, 16384], P(None, 'row'), may hold values from -0.09375 to 0.09375
- down_weight: bfloat16 [16384, 4096], P('row'), may hold values from -0.046875 to 0.046875
- final_gain: float32 [4096], replicated, may hold values from 0.1 to 1.9
- key_weight: bfloat16 [4096, 16384], P(None, 'row'), may hold values from -0.09375 to 0.09375
- value_weight: bfloat16 [4096, 16384], P(None, 'row'), may hold values from -0.09375 to 0.09375
Outputs:
- key_cache: bfloat16 [256, 4, 4096], P(('groups', 'row')), parts along dimension 0
- value_cache: bfloat16 [256, 4, 4096], P(('groups', 'row')), parts along dimension 0
The draws below stay inside these ranges and needn't reach their ends.
There are 2 independent parts, one for each index of `groups`. The reference program is written for one: setup_inputs(seed, part) draws one part's arguments, and reference() takes and returns one part's arrays. A program takes and returns all parts, laid end to end along the dimension named above; an argument that names none is the same for every part. Nothing has to cross between parts.
All inputs are finite; a program needn't handle non-finite values.
Results may differ from the reference program's by a relative error of at most 0.0057.
Values may be sent and summed in bfloat16 or wider, within the bound.
No kernel may reach another device: no remote copies, remote signals or barrier semaphores. Data moves between devices by JAX's collectives and lax.ppermute only.
A program may use at most 128 MiB of HBM per device.

```python
import jax
import jax.numpy as jnp
from jax import lax

D = 4096
FF = 16384
LAYERS = 4
TOK_DEV = 8
TOKENS = 128


def draw_source_slab(key, part):
    first_key, second_key, third_key = jax.random.split(key, 3)
    row_scale = jnp.exp(jax.random.uniform(second_key, (TOKENS, 1), jnp.float32, -1.15, 1.15))
    column_scale = jnp.exp(jax.random.uniform(third_key, (1, D), jnp.float32, -1.15, 1.15))
    base_values = jax.random.truncated_normal(first_key, -4.0, 4.0, (TOKENS, D), jnp.float32)
    return (base_values * row_scale * column_scale).astype(jnp.bfloat16)


def shard_levels(key, extent, cuts, low, largest):
    level, own = 1.0, jax.random.fold_in(key, 6)
    for position, shards_of in cuts:
        heights = jnp.exp(jax.random.uniform(jax.random.fold_in(own, position), (shards_of,), jnp.float32, low / len(cuts), largest / len(cuts)))
        level = level * jnp.repeat(heights, extent[position] // shards_of).reshape([-1 if axis == position else 1 for axis in range(len(extent))])
    return level


def gaussian(stream_key, shape, spread, bound, pieces=(), held_as=jnp.bfloat16):
    drawn = jax.random.normal(stream_key, shape, jnp.float32) * spread
    if len(pieces) > 0:
        drawn = shard_levels(stream_key, shape, pieces, -0.22, 0.18) * drawn
    return jnp.clip(drawn, min=-bound, max=bound).astype(held_as)


def setup_inputs(seed: int = 0, part: int = 0) -> dict:
    arg_keys = jax.random.split(jax.random.key(seed), 11)
    own_keys = jax.random.split(jax.random.fold_in(arg_keys[10], part), 11)
    source_slab = draw_source_slab(jax.random.fold_in(jax.random.fold_in(arg_keys[10], part), 71), part)
    slab_index = jax.random.randint(own_keys[1], (1,), 0, 128).astype(jnp.int32)
    cache_slot = jax.random.permutation(own_keys[2], TOKENS).astype(jnp.int32)
    ffn_gain = jnp.clip(1.0 + 0.18 * jax.random.normal(arg_keys[3], (D,), jnp.float32), 0.1, 1.9)
    gate_weight = gaussian(arg_keys[4], (D, FF), D ** -0.5, 0.09375, ((1, 16),))
    up_weight = gaussian(arg_keys[5], (D, FF), D ** -0.5, 0.09375, ((1, 16),))
    down_weight = gaussian(arg_keys[6], (FF, D), FF ** -0.5, 0.046875, ((0, 16),))
    final_gain = jnp.clip(1.0 + 0.18 * jax.random.normal(arg_keys[7], (D,), jnp.float32), 0.1, 1.9)
    key_weight = gaussian(arg_keys[8], (D, LAYERS * D), D ** -0.5, 0.09375, ((1, 16),))
    value_weight = gaussian(arg_keys[9], (D, LAYERS * D), D ** -0.5, 0.09375, ((1, 16),))
    return {"source_slab": source_slab, "slab_index": slab_index, "cache_slot": cache_slot, "ffn_gain": ffn_gain, "gate_weight": gate_weight, "up_weight": up_weight, "down_weight": down_weight, "final_gain": final_gain, "key_weight": key_weight, "value_weight": value_weight}


epsilon = 1e-06

def rms_normalize(values, scales):
    mean_square = lax.optimization_barrier(jnp.mean(values * values, axis=-1, keepdims=True))
    return values * lax.rsqrt(mean_square + epsilon) * scales

def reference(source_slab, slab_index, cache_slot, ffn_gain, gate_weight, up_weight, down_weight, final_gain, key_weight, value_weight):
    source_rows = source_slab.astype(jnp.float32)
    normed = rms_normalize(source_rows, ffn_gain.astype(jnp.float32)).astype(jnp.bfloat16)
    gate = jnp.dot(normed, gate_weight, preferred_element_type=jnp.float32)
    upward = jnp.dot(normed, up_weight, preferred_element_type=jnp.float32)
    hidden = (jax.nn.silu(gate) * upward).astype(jnp.bfloat16)
    mixed = jnp.dot(hidden, down_weight, preferred_element_type=jnp.float32)
    encoded = rms_normalize(source_rows + mixed, final_gain.astype(jnp.float32)).astype(jnp.bfloat16)
    cache_row = ((cache_slot + slab_index[0] * TOK_DEV) % TOKENS).astype(jnp.int32)
    source_order = jnp.zeros((TOKENS,), jnp.int32).at[cache_row].set(jnp.arange(TOKENS, dtype=jnp.int32))
    placed = encoded[source_order]
    keys = jnp.dot(placed, key_weight, preferred_element_type=jnp.float32).astype(jnp.bfloat16)
    values = jnp.dot(placed, value_weight, preferred_element_type=jnp.float32).astype(jnp.bfloat16)
    return (keys.reshape(TOKENS, LAYERS, D), values.reshape(TOKENS, LAYERS, D))
```

```python
import functools

import jax
import jax.numpy as jnp
from jax import lax
from jax.experimental import pallas as pl
from jax.experimental.pallas import tpu as pltpu
from jax.sharding import PartitionSpec as P

epsilon = 1e-06
f32 = jnp.float32
bf16 = jnp.bfloat16
vmem_limit = 60 * 1024 * 1024


def factor(devices):
    core = 2 if devices % 2 == 0 else 1
    mid = 2 if devices % (2 * core) == 0 else 1
    return devices // (core * mid), mid, core


def shift_perm(devices, step):
    outer, mid, core = factor(devices)
    stride = mid * core
    return [(i, (i - step * stride) % devices) for i in range(devices)]


def xor_perm(devices, bit):
    return [(i, i ^ bit) for i in range(devices)]


def gather_rows(block, devices):
    outer, mid, core = factor(devices)
    parts = [block]
    for step in range(1, outer):
        parts.append(lax.ppermute(block, "row", shift_perm(devices, step)))
    own = jnp.concatenate(parts, axis=0)
    other = lax.ppermute(own, "row", xor_perm(devices, core))
    own_pair = lax.ppermute(own, "row", xor_perm(devices, 1))
    other_pair = lax.ppermute(other, "row", xor_perm(devices, 1))
    return own, other, own_pair, other_pair


def ffn_kernel(
    a_ref, b_ref, c_ref, d_ref, gain_ref, gate_ref, up_ref, down_ref,
    own_out, other_out, own_pair_out, other_pair_out, normed, total,
):
    step = pl.program_id(0)
    rows = a_ref.shape[0]

    @pl.when(step == 0)
    def _():
        for at, ref in enumerate((a_ref, b_ref, c_ref, d_ref)):
            values = ref[...].astype(f32)
            mean_square = jnp.mean(values * values, axis=-1, keepdims=True)
            scaled = values * lax.rsqrt(mean_square + epsilon) * gain_ref[...]
            normed[pl.ds(at * rows, rows), :] = scaled.astype(bf16)

    gate = jnp.dot(normed[...], gate_ref[...], preferred_element_type=f32)
    upward = jnp.dot(normed[...], up_ref[...], preferred_element_type=f32)
    hidden = (gate / (1.0 + jnp.exp(-gate)) * upward).astype(bf16)
    term = jnp.dot(hidden, down_ref[...], preferred_element_type=f32)

    @pl.when(step == 0)
    def _():
        total[...] = term

    @pl.when(step > 0)
    def _():
        total[...] += term

    @pl.when(step == pl.num_programs(0) - 1)
    def _():
        outs = (own_out, other_out, own_pair_out, other_pair_out)
        for at, ref in enumerate(outs):
            ref[...] = total[pl.ds(at * rows, rows), :].astype(ref.dtype)


def ffn(blocks, gain, gate_weight, up_weight, down_weight):
    rows, width = blocks[0].shape
    units = gate_weight.shape[1]
    tile = min(256, units)
    whole = pl.BlockSpec((rows, width), lambda i: (0, 0))
    return pl.pallas_call(
        ffn_kernel,
        grid=(units // tile,),
        in_specs=[whole] * 4
        + [
            pl.BlockSpec((1, width), lambda i: (0, 0)),
            pl.BlockSpec((width, tile), lambda i: (0, i)),
            pl.BlockSpec((width, tile), lambda i: (0, i)),
            pl.BlockSpec((tile, width), lambda i: (i, 0)),
        ],
        out_specs=[whole] * 4,
        out_shape=[
            jax.ShapeDtypeStruct((rows, width), f32),
            jax.ShapeDtypeStruct((rows, width), f32),
            jax.ShapeDtypeStruct((rows, width), bf16),
            jax.ShapeDtypeStruct((rows, width), bf16),
        ],
        scratch_shapes=[
            pltpu.VMEM((4 * rows, width), bf16),
            pltpu.VMEM((4 * rows, width), f32),
        ],
        compiler_params=pltpu.CompilerParams(vmem_limit_bytes=vmem_limit),
        name="ffn",
    )(*blocks, gain.reshape(1, width), gate_weight, up_weight, down_weight)


def whole_call(kernel, out_shapes, name, *args):
    spec = pl.BlockSpec(memory_space=pltpu.VMEM)
    return pl.pallas_call(
        kernel,
        in_specs=[spec] * len(args),
        out_specs=[spec] * len(out_shapes),
        out_shape=out_shapes,
        name=name,
    )(*args)


def add_kernel(a_ref, b_ref, o_ref):
    o_ref[...] = (a_ref[...] + b_ref[...].astype(f32)).astype(bf16)


def split_kernel(a_ref, b_ref, c_ref, kept_ref, *send_refs):
    rows = kept_ref.shape[0]
    for at, ref in enumerate((kept_ref,) + send_refs):
        part = pl.ds(at * rows, rows)
        total = a_ref[part, :] + b_ref[part, :].astype(f32) + c_ref[part, :].astype(f32)
        ref[...] = total.astype(ref.dtype)


def state_kernel(source_ref, gain_ref, kept_ref, *refs):
    state = source_ref[...].astype(f32) + kept_ref[...]
    for ref in refs[:-1]:
        state = state + ref[...].astype(f32)
    refs[-1][...] = (state * gain_ref[...]).astype(bf16)


def project_kernel(
    devices, place_ref, a_ref, b_ref, c_ref, d_ref, gain_ref, slot_ref, key_ref, value_ref,
    out_ref, placed, scale,
):
    step = pl.program_id(0)
    outer, mid, core = factor(devices)
    rows, width = a_ref.shape
    total = 4 * rows
    each = rows // outer

    @pl.when(step == 0)
    def _():
        me, slab = place_ref[0], place_ref[1]
        my_outer, my_mid, my_core = me // (mid * core), (me // core) % mid, me % core
        shape = (total, total)
        first = lax.broadcasted_iota(jnp.int32, shape, 0)
        second = lax.broadcasted_iota(jnp.int32, shape, 1)
        cache_row = lax.rem(slot_ref[...] + slab * each, total)
        to_cache = (cache_row == first).astype(bf16)
        block = second // rows
        at_mid = my_mid ^ (block % 2)
        at_core = my_core ^ (block // 2)
        at_outer = lax.rem(my_outer + (second % rows) // each, outer)
        token = ((at_outer * mid + at_mid) * core + at_core) * each + second % each
        from_order = (token == first).astype(bf16)
        select = jnp.dot(to_cache, from_order, preferred_element_type=f32).astype(bf16)
        inverse = 1.0 / (gain_ref[...] * gain_ref[...])
        ordered = jnp.concatenate([ref[...] for ref in (a_ref, b_ref, c_ref, d_ref)], axis=0)
        moved = jnp.dot(select, ordered, preferred_element_type=f32)
        placed[...] = moved.astype(bf16)
        mean_square = jnp.sum(moved * moved * inverse, axis=-1, keepdims=True) / width
        scale[...] = jnp.broadcast_to(lax.rsqrt(mean_square + epsilon), scale.shape)

    tile = key_ref.shape[1]
    half = out_ref.shape[-1] // 2
    for base, weight in ((0, key_ref), (half, value_ref)):
        product = jnp.dot(placed[...], weight[...], preferred_element_type=f32)
        product = (product * scale[:, :1]).astype(bf16)
        columns = pl.ds(pl.multiple_of(base + step * tile, tile), tile)
        out_ref[:, columns] = product


def project(blocks, place, gain, slot, key_weight, value_weight, devices):
    rows, width = blocks[0].shape
    columns = key_weight.shape[1]
    tile = min(256, columns)
    whole = pl.BlockSpec((rows, width), lambda i: (0, 0))
    return pl.pallas_call(
        functools.partial(project_kernel, devices),
        grid=(columns // tile,),
        in_specs=[pl.BlockSpec(memory_space=pltpu.SMEM)]
        + [whole] * 4
        + [
            pl.BlockSpec((1, width), lambda i: (0, 0)),
            pl.BlockSpec((1, 4 * rows), lambda i: (0, 0)),
            pl.BlockSpec((width, tile), lambda i: (0, i)),
            pl.BlockSpec((width, tile), lambda i: (0, i)),
        ],
        out_specs=pl.BlockSpec((4 * rows, 2 * columns), lambda i: (0, 0)),
        out_shape=jax.ShapeDtypeStruct((4 * rows, 2 * columns), bf16),
        scratch_shapes=[
            pltpu.VMEM((4 * rows, width), bf16),
            pltpu.VMEM((4 * rows, 128), f32),
        ],
        compiler_params=pltpu.CompilerParams(vmem_limit_bytes=vmem_limit),
        name="project",
    )(place, *blocks, gain.reshape(1, width), slot.reshape(1, 4 * rows), key_weight, value_weight)


def on_device(
    source_slab,
    slab_index,
    cache_slot,
    ffn_gain,
    gate_weight,
    up_weight,
    down_weight,
    final_gain,
    key_weight,
    value_weight,
):
    each, width = source_slab.shape
    devices = lax.axis_size("row")
    outer, mid, core = factor(devices)
    me = lax.axis_index("row").astype(jnp.int32)
    place = jnp.stack([me, slab_index[0]])

    blocks = gather_rows(source_slab, devices)
    own, other, own_pair, other_pair = ffn(blocks, ffn_gain, gate_weight, up_weight, down_weight)

    from_pair_other = lax.ppermute(other_pair, "row", xor_perm(devices, 1))
    from_pair_own = lax.ppermute(own_pair, "row", xor_perm(devices, 1))
    rows = own.shape[0]
    (sent,) = whole_call(
        add_kernel, [jax.ShapeDtypeStruct((rows, width), bf16)], "add", other, from_pair_other
    )
    from_mid = lax.ppermute(sent, "row", xor_perm(devices, core))
    kept, *sends = whole_call(
        split_kernel,
        [jax.ShapeDtypeStruct((each, width), f32)]
        + [jax.ShapeDtypeStruct((each, width), bf16)] * (outer - 1),
        "split",
        own,
        from_pair_own,
        from_mid,
    )
    received = [
        lax.ppermute(part, "row", shift_perm(devices, -(step + 1)))
        for step, part in enumerate(sends)
    ]
    (scaled,) = whole_call(
        state_kernel,
        [jax.ShapeDtypeStruct((each, width), bf16)],
        "state",
        source_slab,
        final_gain.reshape(1, width),
        kept,
        *received,
    )
    blocks = gather_rows(scaled, devices)
    out = project(blocks, place, final_gain, cache_slot, key_weight, value_weight, devices)
    columns = key_weight.shape[1]
    layer_count = columns * devices // width
    out = out.reshape(devices, each, 2 * columns)
    out = lax.all_to_all(out, "row", split_axis=0, concat_axis=0, tiled=True)
    out = jnp.transpose(out, (1, 0, 2))
    key_cache = out[:, :, :columns].reshape(each, layer_count, width)
    value_cache = out[:, :, columns:].reshape(each, layer_count, width)
    return (key_cache, value_cache)


def solution(mesh):
    placed = (
        P(("groups", "row"), None),
        P("groups"),
        P("groups"),
        P(),
        P(None, "row"),
        P(None, "row"),
        P("row", None),
        P(),
        P(None, "row"),
        P(None, "row"),
    )
    return jax.shard_map(
        on_device,
        mesh=mesh,
        in_specs=placed,
        out_specs=(P(("groups", "row"), None, None), P(("groups", "row"), None, None)),
        check_vma=False,
    )
```

```python
import functools

import jax
import jax.numpy as jnp
from jax import lax
from jax.experimental import pallas as pl
from jax.experimental.pallas import tpu as pltpu
from jax.sharding import PartitionSpec as P

epsilon = 1e-06
f32 = jnp.float32
bf16 = jnp.bfloat16


def factor(devices):
    core = 2 if devices % 2 == 0 else 1
    mid = 2 if devices % (2 * core) == 0 else 1
    return devices // (core * mid), mid, core


def shift_perm(devices, step):
    _, mid, core = factor(devices)
    stride = mid * core
    return [(i, (i - step * stride) % devices) for i in range(devices)]


def xor_perm(devices, bit):
    return [(i, i ^ bit) for i in range(devices)]


def resident(array):
    return pltpu.with_memory_space_constraint(array, pltpu.VMEM)


def local_call(kernel, out_shapes, *args, scalars=(), scratch=(), limit=8, cost=None):
    vmem = pl.BlockSpec(memory_space=pltpu.VMEM)
    smem = pl.BlockSpec(memory_space=pltpu.SMEM)
    return pl.pallas_call(
        kernel,
        in_specs=[smem] * len(scalars) + [vmem] * len(args),
        out_specs=[vmem] * len(out_shapes),
        out_shape=out_shapes,
        scratch_shapes=list(scratch),
        compiler_params=pltpu.CompilerParams(vmem_limit_bytes=limit * 1024 * 1024),
        cost_estimate=cost,
    )(*scalars, *(resident(arg) for arg in args))


def load_kernel(source_ref, target_ref, arrived):
    rows = source_ref.shape[0]
    pieces = arrived.shape[0]
    copies = []
    for at in range(pieces):
        part = pl.ds(at * (rows // pieces), rows // pieces)
        copies.append(
            pltpu.make_async_copy(source_ref.at[part], target_ref.at[part], arrived.at[at])
        )
    for copy in copies:
        copy.start()
    for copy in copies:
        copy.wait()


def load(array):
    size = array.size * array.dtype.itemsize
    return pl.pallas_call(
        load_kernel,
        in_specs=[pl.BlockSpec(memory_space=pl.ANY)],
        out_specs=pl.BlockSpec(memory_space=pltpu.VMEM),
        out_shape=pltpu.VMEM(array.shape, array.dtype),
        scratch_shapes=[pltpu.SemaphoreType.DMA((4,))],
        compiler_params=pltpu.CompilerParams(vmem_limit_bytes=1024 * 1024),
        cost_estimate=pl.CostEstimate(flops=0, bytes_accessed=size, transcendentals=0),
    )(pltpu.with_memory_space_constraint(array, pltpu.HBM))


def join_kernel(*refs):
    rows = refs[0].shape[0]
    for at, ref in enumerate(refs[:-1]):
        refs[-1][pl.ds(at * rows, rows), :] = ref[...]


def move(array, pairs):
    return lax.ppermute(array, "row", pairs)


def gather_rows(block, devices):
    outer, _, core = factor(devices)
    rows, width = block.shape
    parts = [block]
    for step in range(1, outer):
        parts.append(move(block, shift_perm(devices, step)))
    (own,) = local_call(join_kernel, [pltpu.VMEM((outer * rows, width), block.dtype)], *parts)
    other = move(own, xor_perm(devices, core))
    own_pair = move(own, xor_perm(devices, 1))
    other_pair = move(other, xor_perm(devices, 1))
    return own, other, own_pair, other_pair


def ffn_kernel(
    a_ref, b_ref, c_ref, d_ref, gain_ref, gate_ref, up_ref, down_ref,
    own_out, other_out, own_pair_out, other_pair_out, normed, total,
):
    rows = a_ref.shape[0]
    units = gate_ref.shape[1]
    tile = min(256, units)
    for at, ref in enumerate((a_ref, b_ref, c_ref, d_ref)):
        values = ref[...].astype(f32)
        mean_square = jnp.mean(values * values, axis=-1, keepdims=True)
        scaled = values * lax.rsqrt(mean_square + epsilon) * gain_ref[...]
        normed[pl.ds(at * rows, rows), :] = scaled.astype(bf16)

    def term(step):
        part = pl.ds(pl.multiple_of(step * tile, tile), tile)
        gate = jnp.dot(normed[...], gate_ref[:, part], preferred_element_type=f32)
        upward = jnp.dot(normed[...], up_ref[:, part], preferred_element_type=f32)
        hidden = (gate / (1.0 + jnp.exp(-gate)) * upward).astype(bf16)
        return jnp.dot(hidden, down_ref[part, :], preferred_element_type=f32)

    total[...] = term(0)

    @pl.loop(1, units // tile)
    def _(step):
        total[...] += term(step)

    outs = (own_out, other_out, own_pair_out, other_pair_out)
    for at, ref in enumerate(outs):
        ref[...] = total[pl.ds(at * rows, rows), :].astype(ref.dtype)


def ffn(blocks, gain, gate_weight, up_weight, down_weight):
    rows, width = blocks[0].shape
    units = gate_weight.shape[1]
    return local_call(
        ffn_kernel,
        [
            pltpu.VMEM((rows, width), f32),
            pltpu.VMEM((rows, width), f32),
            pltpu.VMEM((rows, width), bf16),
            pltpu.VMEM((rows, width), bf16),
        ],
        *blocks,
        gain.reshape(1, width),
        gate_weight,
        up_weight,
        down_weight,
        scratch=[pltpu.VMEM((4 * rows, width), bf16), pltpu.VMEM((4 * rows, width), f32)],
        limit=8 if rows <= 32 else 24,
        cost=pl.CostEstimate(
            flops=24 * rows * width * units, bytes_accessed=6 * width * units, transcendentals=0
        ),
    )


def add_kernel(a_ref, b_ref, o_ref):
    o_ref[...] = (a_ref[...] + b_ref[...].astype(f32)).astype(bf16)


def split_kernel(a_ref, b_ref, c_ref, kept_ref, *send_refs):
    rows = kept_ref.shape[0]
    for at, ref in enumerate((kept_ref,) + send_refs):
        part = pl.ds(at * rows, rows)
        total = a_ref[part, :] + b_ref[part, :].astype(f32) + c_ref[part, :].astype(f32)
        ref[...] = total.astype(ref.dtype)


def state_kernel(source_ref, gain_ref, kept_ref, *refs):
    state = source_ref[...].astype(f32) + kept_ref[...]
    for ref in refs[:-1]:
        state = state + ref[...].astype(f32)
    refs[-1][...] = (state * gain_ref[...]).astype(bf16)


def project_kernel(
    devices, slab_ref, a_ref, b_ref, c_ref, d_ref, gain_ref, slot_ref, key_ref, value_ref,
    out_ref, placed, scale,
):
    outer, mid, core = factor(devices)
    rows, width = a_ref.shape
    total = 4 * rows
    each = rows // outer
    me, slab = lax.axis_index("row"), slab_ref[0]
    my_outer, my_mid, my_core = me // (mid * core), (me // core) % mid, me % core
    shape = (total, total)
    first = lax.broadcasted_iota(jnp.int32, shape, 0)
    second = lax.broadcasted_iota(jnp.int32, shape, 1)
    cache_row = lax.rem(slot_ref[...] + slab * each, total)
    to_cache = (cache_row == first).astype(bf16)
    block = second // rows
    at_mid = my_mid ^ (block % 2)
    at_core = my_core ^ (block // 2)
    at_outer = lax.rem(my_outer + (second % rows) // each, outer)
    token = ((at_outer * mid + at_mid) * core + at_core) * each + second % each
    from_order = (token == first).astype(bf16)
    select = jnp.dot(to_cache, from_order, preferred_element_type=f32).astype(bf16)
    inverse = 1.0 / (gain_ref[...] * gain_ref[...])
    ordered = jnp.concatenate([ref[...] for ref in (a_ref, b_ref, c_ref, d_ref)], axis=0)
    moved = jnp.dot(select, ordered, preferred_element_type=f32)
    placed[...] = moved.astype(bf16)
    mean_square = jnp.sum(moved * moved * inverse, axis=-1, keepdims=True) / width
    scale[...] = jnp.broadcast_to(lax.rsqrt(mean_square + epsilon), scale.shape)

    columns = key_ref.shape[1]
    tile = min(256, columns)

    @pl.loop(0, columns // tile)
    def _(step):
        start = pl.multiple_of(step * tile, tile)
        for base, weight in ((0, key_ref), (columns, value_ref)):
            product = jnp.dot(placed[...], weight[:, pl.ds(start, tile)], preferred_element_type=f32)
            product = (product * scale[:, :1]).astype(bf16)
            out_ref[:, pl.ds(pl.multiple_of(base + start, tile), tile)] = product


def project(blocks, slab_index, gain, slot, key_weight, value_weight, devices):
    rows, width = blocks[0].shape
    columns = key_weight.shape[1]
    (out,) = local_call(
        functools.partial(project_kernel, devices),
        [pltpu.VMEM((4 * rows, 2 * columns), bf16)],
        *blocks,
        gain.reshape(1, width),
        slot.reshape(1, 4 * rows),
        key_weight,
        value_weight,
        scalars=(slab_index,),
        scratch=[pltpu.VMEM((4 * rows, width), bf16), pltpu.VMEM((4 * rows, 128), f32)],
        limit=8 if rows <= 32 else 24,
        cost=pl.CostEstimate(
            flops=16 * rows * width * columns, bytes_accessed=4 * width * columns, transcendentals=0
        ),
    )
    return out


def on_device(
    source_slab,
    slab_index,
    cache_slot,
    ffn_gain,
    gate_weight,
    up_weight,
    down_weight,
    final_gain,
    key_weight,
    value_weight,
):
    each, width = source_slab.shape
    devices = lax.axis_size("row")
    outer, _, core = factor(devices)

    gate_weight = load(gate_weight)
    up_weight = load(up_weight)
    down_weight = load(down_weight)
    key_weight = load(key_weight)
    value_weight = load(value_weight)

    blocks = gather_rows(source_slab, devices)
    own, other, own_pair, other_pair = ffn(blocks, ffn_gain, gate_weight, up_weight, down_weight)

    from_pair_other = move(other_pair, xor_perm(devices, 1))
    from_pair_own = move(own_pair, xor_perm(devices, 1))
    rows = own.shape[0]
    (sent,) = local_call(add_kernel, [pltpu.VMEM((rows, width), bf16)], other, from_pair_other)
    from_mid = move(sent, xor_perm(devices, core))
    kept, *sends = local_call(
        split_kernel,
        [pltpu.VMEM((each, width), f32)]
        + [pltpu.VMEM((each, width), bf16)] * (outer - 1),
        own,
        from_pair_own,
        from_mid,
    )
    received = [move(part, shift_perm(devices, -(step + 1))) for step, part in enumerate(sends)]
    (scaled,) = local_call(
        state_kernel,
        [pltpu.VMEM((each, width), bf16)],
        source_slab,
        final_gain.reshape(1, width),
        kept,
        *received,
    )
    blocks = gather_rows(scaled, devices)
    out = project(blocks, slab_index, final_gain, cache_slot, key_weight, value_weight, devices)
    columns = key_weight.shape[1]
    layer_count = columns * devices // width
    out = out.reshape(devices, each, 2 * columns)
    out = lax.all_to_all(out, "row", split_axis=0, concat_axis=0, tiled=True)
    out = jnp.transpose(out, (1, 0, 2))
    key_cache = out[:, :, :columns].reshape(each, layer_count, width)
    value_cache = out[:, :, columns:].reshape(each, layer_count, width)
    return (key_cache, value_cache)


def solution(mesh):
    placed = (
        P(("groups", "row"), None),
        P("groups"),
        P("groups"),
        P(),
        P(None, "row"),
        P(None, "row"),
        P("row", None),
        P(),
        P(None, "row"),
        P(None, "row"),
    )
    return jax.shard_map(
        on_device,
        mesh=mesh,
        in_specs=placed,
        out_specs=(P(("groups", "row"), None, None), P(("groups", "row"), None, None)),
        check_vma=False,
    )
```

```python
import functools

import jax
import jax.numpy as jnp
from jax import lax
from jax.experimental import pallas as pl
from jax.experimental.pallas import tpu as pltpu
from jax.sharding import PartitionSpec as P

epsilon = 1e-06
f32 = jnp.float32
bf16 = jnp.bfloat16


def factor(devices):
    core = 2 if devices % 2 == 0 else 1
    mid = 2 if devices % (2 * core) == 0 else 1
    return devices // (core * mid), mid, core


def shift_perm(devices, step):
    _, mid, core = factor(devices)
    stride = mid * core
    return [(i, (i - step * stride) % devices) for i in range(devices)]


def cross_perm(devices, step):
    _, mid, core = factor(devices)
    stride = mid * core
    return [(i, ((i + step * stride) % devices) ^ core) for i in range(devices)]


def xor_perm(devices, bit):
    return [(i, i ^ bit) for i in range(devices)]


def resident(array):
    return pltpu.with_memory_space_constraint(array, pltpu.VMEM)


def local_call(kernel, out_shapes, *args, scalars=(), scratch=(), limit=8, cost=None):
    vmem = pl.BlockSpec(memory_space=pltpu.VMEM)
    smem = pl.BlockSpec(memory_space=pltpu.SMEM)
    return pl.pallas_call(
        kernel,
        in_specs=[smem] * len(scalars) + [vmem] * len(args),
        out_specs=[vmem] * len(out_shapes),
        out_shape=out_shapes,
        scratch_shapes=list(scratch),
        compiler_params=pltpu.CompilerParams(vmem_limit_bytes=limit * 1024 * 1024),
        cost_estimate=cost,
    )(*scalars, *(resident(arg) for arg in args))


def load_kernel(source_ref, target_ref, arrived):
    rows = source_ref.shape[0]
    pieces = arrived.shape[0]
    copies = []
    for at in range(pieces):
        part = pl.ds(at * (rows // pieces), rows // pieces)
        copies.append(
            pltpu.make_async_copy(source_ref.at[part], target_ref.at[part], arrived.at[at])
        )
    for copy in copies:
        copy.start()
    for copy in copies:
        copy.wait()


def load(array):
    size = array.size * array.dtype.itemsize
    return pl.pallas_call(
        load_kernel,
        in_specs=[pl.BlockSpec(memory_space=pl.ANY)],
        out_specs=pl.BlockSpec(memory_space=pltpu.VMEM),
        out_shape=pltpu.VMEM(array.shape, array.dtype),
        scratch_shapes=[pltpu.SemaphoreType.DMA((4,))],
        compiler_params=pltpu.CompilerParams(vmem_limit_bytes=1024 * 1024),
        cost_estimate=pl.CostEstimate(flops=0, bytes_accessed=size, transcendentals=0),
    )(pltpu.with_memory_space_constraint(array, pltpu.HBM))


def join_kernel(groups, *refs):
    outs = refs[len(refs) - len(groups):]
    for out, group in zip(outs, groups):
        rows = 0
        for at in group:
            size = refs[at].shape[0]
            out[pl.ds(rows, size), :] = refs[at][...]
            rows += size


def join(groups, *parts):
    width = parts[0].shape[1]
    shapes = [
        pltpu.VMEM((sum(parts[at].shape[0] for at in group), width), parts[0].dtype)
        for group in groups
    ]
    return local_call(functools.partial(join_kernel, groups), shapes, *parts)


def move(array, pairs):
    return lax.ppermute(array, "row", pairs)


def gather_own(block, devices):
    outer, _, core = factor(devices)
    parts = [block]
    for step in range(1, outer):
        parts.append(move(block, shift_perm(devices, step)))
    other_first = move(block, xor_perm(devices, core))
    own, rest = join((tuple(range(outer)), tuple(range(1, outer))), *parts, other_first)
    other_rest = move(rest, xor_perm(devices, core))
    own_pair = move(own, xor_perm(devices, 1))
    return own, own_pair, other_first, other_rest


def gather_other(other_first, other_rest, devices):
    (other,) = join(((0, 1),), other_first, other_rest)
    return other, move(other, xor_perm(devices, 1))


def relative_row(position, each, outer, mid, core):
    me = lax.axis_index("row")
    my_outer, my_mid, my_core = me // (mid * core), (me // core) % mid, me % core
    rows = outer * each
    block = position // rows
    at_mid = my_mid ^ (block % 2)
    at_core = my_core ^ (block // 2)
    at_outer = lax.rem(my_outer + (position % rows) // each, outer)
    return ((at_outer * mid + at_mid) * core + at_core) * each + position % each


def ffn_kernel(
    devices, slab_ref, a_ref, b_ref, c_ref, d_ref, slot_ref, gain_ref, gate_ref, up_ref, down_ref,
    source_out, own_out, other_out, own_pair_out, other_pair_out, normed, total,
):
    outer, mid, core = factor(devices)
    rows = a_ref.shape[0]
    count = 4 * rows
    each = rows // outer
    units = gate_ref.shape[1]
    tile = min(256, units)
    for at, ref in enumerate((a_ref, b_ref, c_ref, d_ref)):
        normed[pl.ds(at * rows, rows), :] = ref[...]
    first = lax.broadcasted_iota(jnp.int32, (count, count), 0)
    second = lax.broadcasted_iota(jnp.int32, (count, count), 1)
    cache_row = lax.rem(slot_ref[...] + slab_ref[0] * each, count)
    wanted = (cache_row == relative_row(first, each, outer, mid, core)).astype(bf16)
    held = (first == relative_row(second, each, outer, mid, core)).astype(bf16)
    select = jnp.dot(wanted, held, preferred_element_type=f32).astype(bf16)
    total[...] = jnp.dot(select, normed[...], preferred_element_type=f32)
    source_out[...] = total[pl.ds(0, each), :]
    for at in range(4):
        part = pl.ds(at * rows, rows)
        values = total[part, :]
        mean_square = jnp.mean(values * values, axis=-1, keepdims=True)
        scaled = values * lax.rsqrt(mean_square + epsilon) * gain_ref[...]
        normed[part, :] = scaled.astype(bf16)

    def term(step):
        part = pl.ds(pl.multiple_of(step * tile, tile), tile)
        gate = jnp.dot(normed[...], gate_ref[:, part], preferred_element_type=f32)
        upward = jnp.dot(normed[...], up_ref[:, part], preferred_element_type=f32)
        hidden = (gate / (1.0 + jnp.exp(-gate)) * upward).astype(bf16)
        return jnp.dot(hidden, down_ref[part, :], preferred_element_type=f32)

    total[...] = term(0)

    @pl.loop(1, units // tile)
    def _(step):
        total[...] += term(step)

    outs = (own_out, other_out, own_pair_out, other_pair_out)
    for at, ref in enumerate(outs):
        ref[...] = total[pl.ds(at * rows, rows), :].astype(ref.dtype)


def ffn(blocks, slab_index, slot, gain, gate_weight, up_weight, down_weight, devices):
    rows, width = blocks[0].shape
    units = gate_weight.shape[1]
    each = rows // factor(devices)[0]
    return local_call(
        functools.partial(ffn_kernel, devices),
        [
            pltpu.VMEM((each, width), f32),
            pltpu.VMEM((rows, width), f32),
            pltpu.VMEM((rows, width), f32),
            pltpu.VMEM((rows, width), bf16),
            pltpu.VMEM((rows, width), bf16),
        ],
        *blocks,
        slot.reshape(1, 4 * rows),
        gain.reshape(1, width),
        gate_weight,
        up_weight,
        down_weight,
        scalars=(slab_index,),
        scratch=[pltpu.VMEM((4 * rows, width), bf16), pltpu.VMEM((4 * rows, width), f32)],
        limit=8 if rows <= 32 else 24,
        cost=pl.CostEstimate(
            flops=24 * rows * width * units, bytes_accessed=6 * width * units, transcendentals=0
        ),
    )


def add_kernel(a_ref, b_ref, o_ref):
    skip = a_ref.shape[0] - o_ref.shape[0]
    part = pl.ds(skip, o_ref.shape[0])
    o_ref[...] = (a_ref[part, :] + b_ref[part, :].astype(f32)).astype(bf16)


def split_kernel(a_ref, b_ref, c_ref, d_ref, e_ref, kept_ref, late_ref, *send_refs):
    rows = kept_ref.shape[0]
    first = pl.ds(0, rows)
    kept_ref[...] = a_ref[first, :] + b_ref[first, :].astype(f32)
    late_ref[...] = (d_ref[first, :] + e_ref[first, :].astype(f32)).astype(bf16)
    for at, ref in enumerate(send_refs):
        part = pl.ds((at + 1) * rows, rows)
        received = c_ref[pl.ds(at * rows, rows), :].astype(f32)
        ref[...] = (a_ref[part, :] + b_ref[part, :].astype(f32) + received).astype(bf16)


def state_kernel(source_ref, gain_ref, kept_ref, *refs):
    state = source_ref[...] + kept_ref[...]
    for ref in refs[:-1]:
        state = state + ref[...].astype(f32)
    refs[-1][...] = (state * gain_ref[...]).astype(bf16)


def project_kernel(a_ref, b_ref, gain_ref, key_ref, value_ref, keep_ref, send_ref, both, scale):
    rows, width = a_ref.shape
    inverse = 1.0 / (gain_ref[...] * gain_ref[...])
    for at, ref in enumerate((a_ref, b_ref)):
        part = pl.ds(at * rows, rows)
        both[part, :] = ref[...]
        values = ref[...].astype(f32)
        mean_square = jnp.sum(values * values * inverse, axis=-1, keepdims=True) / width
        scale[part, :] = jnp.broadcast_to(
            lax.rsqrt(mean_square + epsilon), (rows, scale.shape[1])
        )
    columns = key_ref.shape[1]
    tile = min(256, columns)

    @pl.loop(0, columns // tile)
    def _(step):
        start = pl.multiple_of(step * tile, tile)
        for base, weight in ((0, key_ref), (columns, value_ref)):
            product = jnp.dot(both[...], weight[:, pl.ds(start, tile)], preferred_element_type=f32)
            product = (product * scale[:, :1]).astype(bf16)
            place = pl.ds(pl.multiple_of(base + start, tile), tile)
            keep_ref[:, place] = product[:rows]
            send_ref[:, place] = product[rows:]


def project(own, pair, gain, key_weight, value_weight):
    rows, width = own.shape
    columns = key_weight.shape[1]
    return local_call(
        project_kernel,
        [pltpu.VMEM((rows, 2 * columns), bf16)] * 2,
        own,
        pair,
        gain.reshape(1, width),
        key_weight,
        value_weight,
        scratch=[pltpu.VMEM((2 * rows, width), bf16), pltpu.VMEM((2 * rows, 128), f32)],
        limit=8 if rows <= 32 else 24,
        cost=pl.CostEstimate(
            flops=8 * rows * width * columns, bytes_accessed=4 * width * columns, transcendentals=0
        ),
    )


def pack_kernel(skip, a_ref, b_ref, *outs):
    rows = outs[0].shape[0] // 2
    for at, ref in enumerate(outs):
        part = pl.ds((at + skip) * rows, rows)
        ref[pl.ds(0, rows), :] = a_ref[part, :]
        ref[pl.ds(rows, rows), :] = b_ref[part, :]


def pack(kept, received, skip, devices):
    outer, _, _ = factor(devices)
    rows, columns = kept.shape
    each = rows // outer
    return local_call(
        functools.partial(pack_kernel, skip),
        [pltpu.VMEM((2 * each, columns), bf16)] * (outer - skip),
        kept,
        received,
    )


def assemble_kernel(devices, *refs):
    outer, mid, core = factor(devices)
    key_out, value_out, flat = refs[-3:]
    kept, received = refs[0], refs[1]
    messages = refs[2:-3]
    each, layers, width = key_out.shape
    columns = kept.shape[1] // 2
    me = lax.axis_index("row")
    my_outer, my_mid, my_core = me // (mid * core), (me // core) % mid, me % core

    def source(step, mid_bit, core_bit):
        at_outer = lax.rem(my_outer - step + outer, outer)
        return (at_outer * mid + (my_mid ^ mid_bit)) * core + (my_core ^ core_bit)

    first, second = pl.ds(0, each), pl.ds(each, each)
    pieces = [(source(0, 0, 0), kept, first), (source(0, 0, 1), received, first)]
    for at, ref in enumerate(messages):
        step, mid_bit = (at + 1, 0) if at < outer - 1 else (at - outer + 1, 1)
        pieces.append((source(step, mid_bit, 0), ref, first))
        pieces.append((source(step, mid_bit, 1), ref, second))
    for base, out in ((0, key_out), (columns, value_out)):
        for owner, ref, part in pieces:
            place = pl.ds(pl.multiple_of(owner * columns, columns), columns)
            flat[:, place] = ref[part, pl.ds(base, columns)].astype(f32)
        for layer in range(layers):
            out[:, layer, :] = flat[:, pl.ds(layer * width, width)].astype(out.dtype)


def assemble(kept, received, messages, layers, width, devices):
    each = messages[0].shape[0] // 2
    out = jax.ShapeDtypeStruct((each, layers, width), bf16)
    return local_call(
        functools.partial(assemble_kernel, devices),
        [out, out],
        kept,
        received,
        *messages,
        scratch=[pltpu.VMEM((each, layers * width), f32)],
    )


def on_device(
    source_slab,
    slab_index,
    cache_slot,
    ffn_gain,
    gate_weight,
    up_weight,
    down_weight,
    final_gain,
    key_weight,
    value_weight,
):
    each, width = source_slab.shape
    devices = lax.axis_size("row")
    outer, _, core = factor(devices)

    gate_weight = load(gate_weight)
    up_weight = load(up_weight)
    down_weight = load(down_weight)
    key_weight = load(key_weight)
    value_weight = load(value_weight)

    own, own_pair, other_first, other_rest = gather_own(source_slab, devices)
    other, other_pair = gather_other(other_first, other_rest, devices)
    source, own, other, own_pair, other_pair = ffn(
        (own, other, own_pair, other_pair),
        slab_index,
        cache_slot,
        ffn_gain,
        gate_weight,
        up_weight,
        down_weight,
        devices,
    )

    from_pair_other = move(other_pair, xor_perm(devices, 1))
    from_pair_own = move(own_pair, xor_perm(devices, 1))
    rows = own.shape[0]
    (rest,) = local_call(
        add_kernel, [pltpu.VMEM((rows - each, width), bf16)], other, from_pair_other
    )
    from_mid = move(rest, xor_perm(devices, core))
    kept, late, *sends = local_call(
        split_kernel,
        [pltpu.VMEM((each, width), f32)] + [pltpu.VMEM((each, width), bf16)] * outer,
        own,
        from_pair_own,
        from_mid,
        other,
        from_pair_other,
    )
    received = [move(part, shift_perm(devices, -(step + 1))) for step, part in enumerate(sends)]
    received.append(move(late, xor_perm(devices, core)))
    (scaled,) = local_call(
        state_kernel,
        [pltpu.VMEM((each, width), bf16)],
        source,
        final_gain.reshape(1, width),
        kept,
        *received,
    )

    own, own_pair, other_first, other_rest = gather_own(scaled, devices)
    near, near_send = project(own, own_pair, final_gain, key_weight, value_weight)
    near_pair = move(near_send, xor_perm(devices, 1))
    messages = [
        move(part, shift_perm(devices, -(step + 1)))
        for step, part in enumerate(pack(near, near_pair, 1, devices))
    ]
    other, other_pair = gather_other(other_first, other_rest, devices)
    far, far_send = project(other, other_pair, final_gain, key_weight, value_weight)
    far_pair = move(far_send, xor_perm(devices, 1))
    messages += [
        move(part, cross_perm(devices, step))
        for step, part in enumerate(pack(far, far_pair, 0, devices))
    ]
    layer_count = key_weight.shape[1] * devices // width
    return tuple(assemble(near, near_pair, messages, layer_count, width, devices))


def solution(mesh):
    placed = (
        P(("groups", "row"), None),
        P("groups"),
        P("groups"),
        P(),
        P(None, "row"),
        P(None, "row"),
        P("row", None),
        P(),
        P(None, "row"),
        P(None, "row"),
    )
    return jax.shard_map(
        on_device,
        mesh=mesh,
        in_specs=placed,
        out_specs=(P(("groups", "row"), None, None), P(("groups", "row"), None, None)),
        check_vma=False,
    )
```

```python
import functools

import jax
import jax.numpy as jnp
from jax import lax
from jax.experimental import pallas as pl
from jax.experimental.pallas import tpu as pltpu
from jax.sharding import PartitionSpec as P

epsilon = 1e-06
f32 = jnp.float32
bf16 = jnp.bfloat16


def factor(devices):
    core = 2 if devices % 2 == 0 else 1
    mid = 2 if devices % (2 * core) == 0 else 1
    return devices // (core * mid), mid, core


def shift_perm(devices, step):
    _, mid, core = factor(devices)
    stride = mid * core
    return [(i, (i - step * stride) % devices) for i in range(devices)]


def cross_perm(devices, step):
    _, mid, core = factor(devices)
    stride = mid * core
    return [(i, ((i + step * stride) % devices) ^ core) for i in range(devices)]


def xor_perm(devices, bit):
    return [(i, i ^ bit) for i in range(devices)]


def resident(array):
    return pltpu.with_memory_space_constraint(array, pltpu.VMEM)


def local_call(kernel, out_shapes, *args, scalars=(), scratch=(), limit=8, cost=None):
    vmem = pl.BlockSpec(memory_space=pltpu.VMEM)
    smem = pl.BlockSpec(memory_space=pltpu.SMEM)
    return pl.pallas_call(
        kernel,
        in_specs=[smem] * len(scalars) + [vmem] * len(args),
        out_specs=[vmem] * len(out_shapes),
        out_shape=out_shapes,
        scratch_shapes=list(scratch),
        compiler_params=pltpu.CompilerParams(vmem_limit_bytes=limit * 1024 * 1024),
        cost_estimate=cost,
    )(*scalars, *(resident(arg) for arg in args))


def load_kernel(ranges, *refs):
    sources, targets, arrived = refs[: len(ranges)], refs[len(ranges) : -1], refs[-1]
    copies = [
        pltpu.make_async_copy(source.at[pl.ds(first, rows)], target, arrived.at[at])
        for at, (source, target, (first, rows)) in enumerate(zip(sources, targets, ranges))
    ]
    for copy in copies:
        copy.start()
    for copy in copies:
        copy.wait()


def load(*parts):
    arrays = [pltpu.with_memory_space_constraint(array, pltpu.HBM) for array, _, _ in parts]
    ranges = tuple((first, rows) for _, first, rows in parts)
    shapes = [pltpu.VMEM((rows, array.shape[1]), array.dtype) for array, _, rows in parts]
    size = sum(rows * array.shape[1] * array.dtype.itemsize for array, _, rows in parts)
    return pl.pallas_call(
        functools.partial(load_kernel, ranges),
        in_specs=[pl.BlockSpec(memory_space=pl.ANY)] * len(parts),
        out_specs=[pl.BlockSpec(memory_space=pltpu.VMEM)] * len(parts),
        out_shape=shapes,
        scratch_shapes=[pltpu.SemaphoreType.DMA((len(parts),))],
        compiler_params=pltpu.CompilerParams(vmem_limit_bytes=1024 * 1024),
        cost_estimate=pl.CostEstimate(flops=0, bytes_accessed=size, transcendentals=0),
    )(*arrays)


def join_kernel(groups, *refs):
    outs = refs[len(refs) - len(groups):]
    for out, group in zip(outs, groups):
        rows = 0
        for at in group:
            size = refs[at].shape[0]
            out[pl.ds(rows, size), :] = refs[at][...]
            rows += size


def join(groups, *parts):
    width = parts[0].shape[1]
    shapes = [
        pltpu.VMEM((sum(parts[at].shape[0] for at in group), width), parts[0].dtype)
        for group in groups
    ]
    return local_call(functools.partial(join_kernel, groups), shapes, *parts)


def move(array, pairs):
    return lax.ppermute(array, "row", pairs)


def gather_own(block, devices):
    outer, _, core = factor(devices)
    parts = [block]
    for step in range(1, outer):
        parts.append(move(block, shift_perm(devices, step)))
    (own,) = join((tuple(range(outer)),), *parts)
    other = move(own, xor_perm(devices, core))
    own_pair = move(own, xor_perm(devices, 1))
    return own, own_pair, other


def gather_other(other, devices):
    return move(other, xor_perm(devices, 1))


def relative_row(position, each, outer, mid, core):
    me = lax.axis_index("row")
    my_outer, my_mid, my_core = me // (mid * core), (me // core) % mid, me % core
    rows = outer * each
    block = position // rows
    at_mid = my_mid ^ (block % 2)
    at_core = my_core ^ (block // 2)
    at_outer = lax.rem(my_outer + (position % rows) // each, outer)
    return ((at_outer * mid + at_mid) * core + at_core) * each + position % each


def ffn_kernel(
    devices, slab_ref, a_ref, b_ref, c_ref, d_ref, slot_ref, gain_ref, gate_ref, up_ref, rest_ref, down_ref,
    source_out, own_out, other_out, own_pair_out, other_pair_out, normed, total,
):
    outer, mid, core = factor(devices)
    rows = a_ref.shape[0]
    count = 4 * rows
    each = rows // outer
    units = gate_ref.shape[1]
    half = up_ref.shape[0]
    tile = min(256, units)
    for at, ref in enumerate((a_ref, b_ref, c_ref, d_ref)):
        normed[pl.ds(at * rows, rows), :] = ref[...]
    first = lax.broadcasted_iota(jnp.int32, (count, count), 0)
    second = lax.broadcasted_iota(jnp.int32, (count, count), 1)
    cache_row = lax.rem(slot_ref[...] + slab_ref[0] * each, count)
    wanted = (cache_row == relative_row(first, each, outer, mid, core)).astype(bf16)
    held = (first == relative_row(second, each, outer, mid, core)).astype(bf16)
    select = jnp.dot(wanted, held, preferred_element_type=f32).astype(bf16)
    total[...] = jnp.dot(select, normed[...], preferred_element_type=f32)
    source_out[...] = total[pl.ds(0, each), :]
    for at in range(4):
        part = pl.ds(at * rows, rows)
        values = total[part, :]
        mean_square = jnp.mean(values * values, axis=-1, keepdims=True)
        scaled = values * lax.rsqrt(mean_square + epsilon) * gain_ref[...]
        normed[part, :] = scaled.astype(bf16)

    def term(step):
        part = pl.ds(pl.multiple_of(step * tile, tile), tile)
        gate = jnp.dot(normed[...], gate_ref[:, part], preferred_element_type=f32)
        upward = jnp.dot(normed[:, :half], up_ref[:, part], preferred_element_type=f32)
        upward += jnp.dot(normed[:, half:], rest_ref[:, part], preferred_element_type=f32)
        hidden = (gate / (1.0 + jnp.exp(-gate)) * upward).astype(bf16)
        return jnp.dot(hidden, down_ref[part, :], preferred_element_type=f32)

    total[...] = term(0)

    @pl.loop(1, units // tile)
    def _(step):
        total[...] += term(step)

    outs = (own_out, other_out, own_pair_out, other_pair_out)
    for at, ref in enumerate(outs):
        ref[...] = total[pl.ds(at * rows, rows), :].astype(ref.dtype)


def ffn(blocks, slab_index, slot, gain, gate_weight, up_weight, up_rest, down_weight, devices):
    rows, width = blocks[0].shape
    units = gate_weight.shape[1]
    each = rows // factor(devices)[0]
    return local_call(
        functools.partial(ffn_kernel, devices),
        [
            pltpu.VMEM((each, width), f32),
            pltpu.VMEM((rows, width), f32),
            pltpu.VMEM((rows, width), f32),
            pltpu.VMEM((rows, width), bf16),
            pltpu.VMEM((rows, width), bf16),
        ],
        *blocks,
        slot.reshape(1, 4 * rows),
        gain.reshape(1, width),
        gate_weight,
        up_weight,
        up_rest,
        down_weight,
        scalars=(slab_index,),
        scratch=[pltpu.VMEM((4 * rows, width), bf16), pltpu.VMEM((4 * rows, width), f32)],
        limit=8 if rows <= 32 else 24,
        cost=pl.CostEstimate(
            flops=24 * rows * width * units, bytes_accessed=6 * width * units, transcendentals=0
        ),
    )


def add_kernel(a_ref, b_ref, o_ref):
    skip = a_ref.shape[0] - o_ref.shape[0]
    part = pl.ds(skip, o_ref.shape[0])
    o_ref[...] = (a_ref[part, :] + b_ref[part, :].astype(f32)).astype(bf16)


def split_kernel(a_ref, b_ref, c_ref, d_ref, e_ref, kept_ref, late_ref, *send_refs):
    rows = kept_ref.shape[0]
    first = pl.ds(0, rows)
    kept_ref[...] = a_ref[first, :] + b_ref[first, :].astype(f32)
    late_ref[...] = (d_ref[first, :] + e_ref[first, :].astype(f32)).astype(bf16)
    for at, ref in enumerate(send_refs):
        part = pl.ds((at + 1) * rows, rows)
        received = c_ref[pl.ds(at * rows, rows), :].astype(f32)
        ref[...] = (a_ref[part, :] + b_ref[part, :].astype(f32) + received).astype(bf16)


def state_kernel(source_ref, gain_ref, kept_ref, *refs):
    state = source_ref[...] + kept_ref[...]
    for ref in refs[:-1]:
        state = state + ref[...].astype(f32)
    refs[-1][...] = (state * gain_ref[...]).astype(bf16)


def project_kernel(a_ref, b_ref, gain_ref, key_ref, value_ref, keep_ref, send_ref, both, scale):
    rows, width = a_ref.shape
    inverse = 1.0 / (gain_ref[...] * gain_ref[...])
    for at, ref in enumerate((a_ref, b_ref)):
        part = pl.ds(at * rows, rows)
        both[part, :] = ref[...]
        values = ref[...].astype(f32)
        mean_square = jnp.sum(values * values * inverse, axis=-1, keepdims=True) / width
        scale[part, :] = jnp.broadcast_to(
            lax.rsqrt(mean_square + epsilon), (rows, scale.shape[1])
        )
    columns = key_ref.shape[1]
    tile = min(256, columns)

    @pl.loop(0, columns // tile)
    def _(step):
        start = pl.multiple_of(step * tile, tile)
        for base, weight in ((0, key_ref), (columns, value_ref)):
            product = jnp.dot(both[...], weight[:, pl.ds(start, tile)], preferred_element_type=f32)
            product = (product * scale[:, :1]).astype(bf16)
            place = pl.ds(pl.multiple_of(base + start, tile), tile)
            keep_ref[:, place] = product[:rows]
            send_ref[:, place] = product[rows:]


def project(own, pair, gain, key_weight, value_weight):
    rows, width = own.shape
    columns = key_weight.shape[1]
    return local_call(
        project_kernel,
        [pltpu.VMEM((rows, 2 * columns), bf16)] * 2,
        own,
        pair,
        gain.reshape(1, width),
        key_weight,
        value_weight,
        scratch=[pltpu.VMEM((2 * rows, width), bf16), pltpu.VMEM((2 * rows, 128), f32)],
        limit=8 if rows <= 32 else 24,
        cost=pl.CostEstimate(
            flops=8 * rows * width * columns, bytes_accessed=4 * width * columns, transcendentals=0
        ),
    )


def pack_kernel(skip, a_ref, b_ref, *outs):
    rows = outs[0].shape[0] // 2
    for at, ref in enumerate(outs):
        part = pl.ds((at + skip) * rows, rows)
        ref[pl.ds(0, rows), :] = a_ref[part, :]
        ref[pl.ds(rows, rows), :] = b_ref[part, :]


def pack(kept, received, skip, devices):
    outer, _, _ = factor(devices)
    rows, columns = kept.shape
    each = rows // outer
    return local_call(
        functools.partial(pack_kernel, skip),
        [pltpu.VMEM((2 * each, columns), bf16)] * (outer - skip),
        kept,
        received,
    )


def assemble_kernel(devices, *refs):
    outer, mid, core = factor(devices)
    key_out, value_out, flat = refs[-3:]
    kept, received = refs[0], refs[1]
    messages = refs[2:-3]
    each, layers, width = key_out.shape
    columns = kept.shape[1] // 2
    me = lax.axis_index("row")
    my_outer, my_mid, my_core = me // (mid * core), (me // core) % mid, me % core

    def source(step, mid_bit, core_bit):
        at_outer = lax.rem(my_outer - step + outer, outer)
        return (at_outer * mid + (my_mid ^ mid_bit)) * core + (my_core ^ core_bit)

    first, second = pl.ds(0, each), pl.ds(each, each)
    pieces = [(source(0, 0, 0), kept, first), (source(0, 0, 1), received, first)]
    for at, ref in enumerate(messages):
        step, mid_bit = (at + 1, 0) if at < outer - 1 else (at - outer + 1, 1)
        pieces.append((source(step, mid_bit, 0), ref, first))
        pieces.append((source(step, mid_bit, 1), ref, second))
    for base, out in ((0, key_out), (columns, value_out)):
        for owner, ref, part in pieces:
            place = pl.ds(pl.multiple_of(owner * columns, columns), columns)
            flat[:, place] = ref[part, pl.ds(base, columns)].astype(f32)
        for layer in range(layers):
            out[:, layer, :] = flat[:, pl.ds(layer * width, width)].astype(out.dtype)


def assemble(kept, received, messages, layers, width, devices):
    each = messages[0].shape[0] // 2
    out = jax.ShapeDtypeStruct((each, layers, width), bf16)
    return local_call(
        functools.partial(assemble_kernel, devices),
        [out, out],
        kept,
        received,
        *messages,
        scratch=[pltpu.VMEM((each, layers * width), f32)],
    )


def on_device(
    source_slab,
    slab_index,
    cache_slot,
    ffn_gain,
    gate_weight,
    up_weight,
    down_weight,
    final_gain,
    key_weight,
    value_weight,
):
    each, width = source_slab.shape
    devices = lax.axis_size("row")
    outer, _, core = factor(devices)

    half = width // 2
    units = down_weight.shape[0]
    gate_weight, up_first = load((gate_weight, 0, width), (up_weight, 0, half))
    up_rest, down_weight = load((up_weight, half, half), (down_weight, 0, units))
    (key_weight,) = load((key_weight, 0, width))
    (value_weight,) = load((value_weight, 0, width))

    own, own_pair, other = gather_own(source_slab, devices)
    other_pair = gather_other(other, devices)
    source, own, other, own_pair, other_pair = ffn(
        (own, other, own_pair, other_pair),
        slab_index,
        cache_slot,
        ffn_gain,
        gate_weight,
        up_first,
        up_rest,
        down_weight,
        devices,
    )

    from_pair_other = move(other_pair, xor_perm(devices, 1))
    from_pair_own = move(own_pair, xor_perm(devices, 1))
    rows = own.shape[0]
    (rest,) = local_call(
        add_kernel, [pltpu.VMEM((rows - each, width), bf16)], other, from_pair_other
    )
    from_mid = move(rest, xor_perm(devices, core))
    kept, late, *sends = local_call(
        split_kernel,
        [pltpu.VMEM((each, width), f32)] + [pltpu.VMEM((each, width), bf16)] * outer,
        own,
        from_pair_own,
        from_mid,
        other,
        from_pair_other,
    )
    received = [move(part, shift_perm(devices, -(step + 1))) for step, part in enumerate(sends)]
    received.append(move(late, xor_perm(devices, core)))
    (scaled,) = local_call(
        state_kernel,
        [pltpu.VMEM((each, width), bf16)],
        source,
        final_gain.reshape(1, width),
        kept,
        *received,
    )

    own, own_pair, other = gather_own(scaled, devices)
    near, near_send = project(own, own_pair, final_gain, key_weight, value_weight)
    near_pair = move(near_send, xor_perm(devices, 1))
    messages = [
        move(part, shift_perm(devices, -(step + 1)))
        for step, part in enumerate(pack(near, near_pair, 1, devices))
    ]
    other_pair = gather_other(other, devices)
    far, far_send = project(other, other_pair, final_gain, key_weight, value_weight)
    far_pair = move(far_send, xor_perm(devices, 1))
    messages += [
        move(part, cross_perm(devices, step))
        for step, part in enumerate(pack(far, far_pair, 0, devices))
    ]
    layer_count = key_weight.shape[1] * devices // width
    return tuple(assemble(near, near_pair, messages, layer_count, width, devices))


def solution(mesh):
    placed = (
        P(("groups", "row"), None),
        P("groups"),
        P("groups"),
        P(),
        P(None, "row"),
        P(None, "row"),
        P("row", None),
        P(),
        P(None, "row"),
        P(None, "row"),
    )
    return jax.shard_map(
        on_device,
        mesh=mesh,
        in_specs=placed,
        out_specs=(P(("groups", "row"), None, None), P(("groups", "row"), None, None)),
        check_vma=False,
    )
```
